256 devices in a mesh: tile: 64 (over x, z, core), pair: 4 (over y).
Axes of the slice: x: 4, y: 4, z: 8, core: 2. Of those that a mesh axis runs over, the one named last changes fastest.
Arguments:
- tokens: bfloat16 [768, 128, 512], P('tile'), may hold values from -64 to 64
- w_query: bfloat16 [512, 512], replicated, may hold values from -4.5 to 4.5
- w_key: bfloat16 [512, 512], replicated, may hold values from -4.5 to 4.5
- w_value: bfloat16 [512, 512], replicated, may hold values from -0.25 to 0.25
- w_out: bfloat16 [512, 512], P(None, 'pair'), may hold values from -0.25 to 0.25
- key_owner: int32 [4, 768, 4], P('pair', 'tile'), may hold values from 0 to 63, all different within a row; in each aligned block of 12 rows (0 to 11, 12 to 23, ..., all dimensions but the last counted through in order) at most 2 rows name the same one
- key_local: int32 [4, 768, 4], P('pair', 'tile'), may hold values from 0 to 11
Outputs:
- attended_out: bfloat16 [768, 128, 512], P('tile', None, 'pair')
The draws below stay inside these ranges and needn't reach their ends.
Inputs may be any that keep to these rules, and one draw needn't show every extreme that they name: `key_owner`: the 4 owners of one row differ; among the 12 rows of one index of tile at one index of pair no owner is named more than 2 times.
All inputs are finite; a program needn't handle non-finite values.
Results may differ from the reference program's by a relative error of at most 0.0045.
The reference program's roundings to bfloat16 on the way count: a program that leaves them out, or rounds other values in their place, can miss the bound.
Values may be sent and summed in bfloat16 or wider, within the bound.
No kernel may reach another device: no remote copies, remote signals or barrier semaphores. Data moves between devices by JAX's collectives and lax.ppermute only.
A program may use at most 128 MiB of HBM per device.

```python
import math
import jax
import jax.numpy as jnp
import numpy as np
from jax import lax

C = 512
GROUPS = 32
TILE = 128
KEYS_DEV = 4
TILES_DEV = 12
TILES = 768
CAP = 2
N_TILE = 64
N_PAIR = 4


def draw_tokens(key, part):
    key_base, key_row, key_col = jax.random.split(jax.random.fold_in(key, 11), 3)
    position = jnp.arange(TILES, dtype=jnp.float32) / max(TILES - 1, 1)
    rising = jnp.exp(jnp.log(3.0) * position)[:, None, None]
    group_scale = jnp.exp(jnp.log(10.0) * jax.random.uniform(key_row, (TILES, TILE, GROUPS, 1), jnp.float32))
    row_scale = jnp.broadcast_to(group_scale, (TILES, TILE, GROUPS, C // GROUPS)).reshape(TILES, TILE, C)
    col_scale = jnp.exp(jnp.log(10.0) * jax.random.uniform(key_col, (1, 1, C), jnp.float32))
    base = jnp.clip(jax.random.normal(key_base, (TILES, TILE, C), jnp.float32), -4.0, 4.0)
    values = base * row_scale * col_scale * rising / 20.0
    return values.astype(jnp.bfloat16)


def projection_draw(key, salt):
    noise = jnp.clip(jax.random.normal(jax.random.fold_in(key, salt), (C, C), jnp.float32), -4.0, 4.0) * C ** (-0.5)
    index = jnp.arange(C)
    identity = (index[:, None] == index[None, :]).astype(jnp.float32)
    noise = noise + 1.5 * identity
    return noise.astype(jnp.bfloat16)


def draw_w_query(key, part):
    return projection_draw(key, 23)


def draw_w_key(key, part):
    return projection_draw(key, 37)


def set_ends(values, rng, least, high):
    dims = values.shape
    place = [jax.random.randint(jax.random.fold_in(rng, axis), (), 0, dims[axis]) for axis in range(len(dims))]
    values = values.at[tuple(place)].set(least)
    longest = dims.index(max(dims))
    place[longest] = (place[longest] + 1) % dims[longest]
    return values.at[tuple(place)].set(high)


def steps_of(rng, shape, pieces, low, high):
    factor_of, own = 1.0, jax.random.fold_in(rng, 6)
    for dim, shards_of in pieces:
        steps = jnp.exp(jax.random.uniform(jax.random.fold_in(own, dim), (shards_of,), jnp.float32, low / len(pieces), high / len(pieces)))
        factor_of = factor_of * jnp.repeat(steps, shape[dim] // shards_of).reshape([-1 if axis == dim else 1 for axis in range(len(shape))])
    return factor_of


def shared_out(rng, own, number, rows, amount, top, bound, skew):
    sequence = jax.random.permutation(rng, amount)
    heavy_load, ordinary = load_shares(amount, rows * top, bound, skew, True), load_shares(amount, rows * top, bound, skew, False)
    places = jnp.arange(amount)

    def named(sizes, rotation):
        used = int((sizes > 0).sum())
        fixed = max(1, used // 4)
        shifted = fixed + (places - fixed + rotation * (used - fixed)) % max(1, amount - fixed)
        return jnp.zeros((amount,), jnp.int32).at[sequence[jnp.where(places < fixed, places, shifted)]].set(jnp.asarray(sizes, jnp.int32))

    sizes = jnp.where(number % 4 == 0, named(heavy_load, number // 4), named(ordinary, number - number // 4 - 1))
    mixed = jax.random.permutation(jax.random.fold_in(own, 3), amount)
    donor, taker = mixed[0:amount // 2 * 2:2], mixed[1:amount // 2 * 2:2]
    margin = jnp.minimum(sizes[donor] - 1, bound - sizes[taker]) // 2
    margin = jnp.where((donor == sequence[0]) | (taker == sequence[0]) | (sizes[taker] == 0), 0, jnp.maximum(margin, 0))
    shifted = jax.random.randint(jax.random.fold_in(own, 4), (amount // 2,), 0, 1 << 20) % (margin + 1)
    sizes = sizes.at[donor].add(-shifted).at[taker].add(shifted)
    labels = jnp.searchsorted(jnp.cumsum(sizes), jnp.arange(rows * top), side="right").astype(jnp.int32)
    grid = labels.reshape(top, rows).T
    grid = grid[jax.random.permutation(jax.random.fold_in(own, 1), rows)]
    rotation = jax.random.randint(jax.random.fold_in(own, 2), (rows, 1), 0, top)
    return jnp.take_along_axis(grid, (jnp.arange(top)[None, :] + rotation) % top, axis=1)


def load_shares(amount, total, bound, skew, full):
    loads = [(1 << 20) // math.isqrt(standing ** skew) + 1 for standing in range(1, amount + 1)]
    largest = bound if full else min(bound, max(-(-total // amount), total * loads[0] // sum(loads)))
    least = 1 if total - largest >= amount - 1 else 0
    given, spare = [largest] + [least] * (amount - 1), total - largest - least * (amount - 1)
    while spare > 0:
        movable = [i for i in range(1, amount) if given[i] < largest] or [i for i in range(1, amount) if given[i] < bound]
        whole, budget = sum([loads[i] for i in movable]), spare
        for i in movable:
            more = min(bound - given[i], max(1, budget * loads[i] // whole), spare)
            given[i] = given[i] + more
            spare = spare - more
    return np.array(given)


def bell_draw(stream_key, extent, scale, limit, pieces=(), kind=jnp.bfloat16):
    factor_of = steps_of(stream_key, extent, pieces, -0.22, 0.18) if pieces else 1.0
    values = jax.random.normal(stream_key, extent, jnp.float32) * scale * factor_of
    return jnp.minimum(jnp.maximum(values, -limit), limit).astype(kind)


def setup_inputs(seed: int = 0) -> dict:
    key_of = jax.random.split(jax.random.key(seed), 8)
    tokens = draw_tokens(jax.random.fold_in(key_of[7], 71), 0)
    w_query = draw_w_query(jax.random.fold_in(key_of[7], 71), 0)
    w_key = draw_w_key(jax.random.fold_in(key_of[7], 71), 0)
    w_value = bell_draw(key_of[3], (C, C), C ** -0.5, 0.25)
    w_out = bell_draw(key_of[4], (C, C), C ** -0.5, 0.25, ((1, 4),))
    key_owner_keys = jax.random.split(jax.random.fold_in(key_of[5], 1), N_PAIR * TILES // TILES_DEV)
    key_owner_turns = jax.random.permutation(jax.random.fold_in(key_of[5], 3), N_PAIR * TILES // TILES_DEV)
    key_owner = jax.vmap(lambda own, number: shared_out(jax.random.fold_in(key_of[5], 2), own, number, TILES_DEV, N_TILE, KEYS_DEV, CAP, 2))(key_owner_keys, key_owner_turns).reshape((N_PAIR, TILES, KEYS_DEV))
    key_local = set_ends(jax.random.randint(key_of[6], (N_PAIR, TILES, KEYS_DEV), 0, TILES_DEV), jax.random.fold_in(key_of[6], 1), 0, TILES_DEV - 1).astype(jnp.int32)
    return {"tokens": tokens, "w_query": w_query, "w_key": w_key, "w_value": w_value, "w_out": w_out, "key_owner": key_owner, "key_local": key_local}


EPS = 1e-06

def reference(tokens, w_query, w_key, w_value, w_out, key_owner, key_local):
    width = C
    grouped = tokens.astype(jnp.float32).reshape(TILES * TILE, GROUPS, width // GROUPS)
    total = lax.optimization_barrier(jnp.sum(grouped, axis=(0, 2)))
    squares = lax.optimization_barrier(jnp.sum(grouped * grouped, axis=(0, 2)))
    count = TILES * TILE * (width // GROUPS)
    mean = total / count
    var = squares / count - mean * mean
    normed = (grouped - mean[None, :, None]) * lax.rsqrt(var + EPS)[None, :, None]
    normed = normed.reshape(TILES * TILE, width).astype(jnp.bfloat16)
    query = jnp.dot(normed, w_query, preferred_element_type=jnp.float32).astype(jnp.bfloat16).reshape(TILES, TILE, width)
    key = jnp.dot(normed, w_key, preferred_element_type=jnp.float32).astype(jnp.bfloat16).reshape(TILES, TILE, width)
    value = jnp.dot(normed, w_value, preferred_element_type=jnp.float32).astype(jnp.bfloat16).reshape(TILES, TILE, width)
    tile_ids = (key_owner * TILES_DEV + key_local).astype(jnp.int32)
    scale = 1.0 / math.sqrt(width)

    def one_block(block):
        start = (block * TILES_DEV).astype(jnp.int32)
        query_blk = lax.dynamic_slice_in_dim(query, start, TILES_DEV, 0).astype(jnp.float32)
        ids_blk = lax.dynamic_slice_in_dim(tile_ids, start, TILES_DEV, 1)
        peaks, masses, parts = ([], [], [])
        for quarter in range(N_PAIR):
            chosen = ids_blk[quarter]
            keys_q = key[chosen].reshape(TILES_DEV, KEYS_DEV * TILE, width).astype(jnp.float32)
            vals_q = value[chosen].reshape(TILES_DEV, KEYS_DEV * TILE, width).astype(jnp.float32)
            scores = jnp.einsum('tqc,tkc->tqk', query_blk, keys_q) * scale
            peak = lax.optimization_barrier(jnp.max(scores, axis=-1, keepdims=True))
            weights = jnp.exp(scores - peak).astype(jnp.bfloat16).astype(jnp.float32)
            peaks.append(peak)
            masses.append(lax.optimization_barrier(jnp.sum(weights, axis=-1, keepdims=True)))
            parts.append(jnp.einsum('tqk,tkc->tqc', weights, vals_q))
        top = peaks[0]
        for item in peaks[1:]:
            top = jnp.maximum(top, item)
        numer = jnp.zeros((TILES_DEV, TILE, width), jnp.float32)
        denom = jnp.zeros((TILES_DEV, TILE, 1), jnp.float32)
        for quarter in range(N_PAIR):
            factor = jnp.exp(peaks[quarter] - top)
            numer = numer + factor * parts[quarter]
            denom = denom + factor * masses[quarter]
        attended = (numer / denom).astype(jnp.bfloat16).reshape(TILES_DEV * TILE, width)
        result = jnp.dot(attended, w_out, preferred_element_type=jnp.float32).astype(jnp.bfloat16)
        return result.reshape(TILES_DEV, TILE, width)
    blocks = lax.map(one_block, jnp.arange(N_TILE, dtype=jnp.int32))
    return blocks.reshape(TILES, TILE, C)
```

```python
import math

import jax
import jax.numpy as jnp
from jax import lax
from jax.experimental import pallas as pl
from jax.experimental.pallas import tpu as pltpu
from jax.sharding import Mesh
from jax.sharding import PartitionSpec as P

GROUPS = 32
EPS = 1e-06
CHUNK = 4
LOW = -1e30
BF = jnp.bfloat16
F32 = jnp.float32
TILE = ("x", "z", "core")


def plan_kernel(tiles, parts, keys, code_ref, slot_ref, row_ref, count_ref):
    size = slot_ref.shape[0]

    def clear(i, _):
        slot_ref[i] = 0
        row_ref[i] = tiles
        return 0

    lax.fori_loop(0, size, clear, 0)

    def one_tile(t, n):
        for p in range(parts):
            for e in range(keys):
                code = code_ref[(p * tiles + t) * keys + e]
                mine = code >= 0
                slot_ref[n] = jnp.where(mine, code, 0)
                row_ref[n] = jnp.where(mine, t, tiles)
                n = n + mine.astype(jnp.int32)
        return n

    count_ref[0] = lax.fori_loop(0, tiles, one_tile, jnp.int32(0))


def split_rows(x):
    high = x.astype(BF)
    rest = x - high.astype(F32)
    mid = rest.astype(BF)
    low = (rest - mid.astype(F32)).astype(BF)
    return [part.astype(F32) for part in (high, mid, low)]


def attend_kernel(
    count_ref, slot_ref, row_ref, own_ref, moments_ref, wq_ref, wk_ref, wv_ref, pool_ref,
    out_ref, held, query, peak, mass, total, sems,
):
    tiles, length, width = own_ref.shape
    lanes = peak.shape[2]
    blocks = width // lanes
    scale = 1.0 / math.sqrt(width)
    mean = moments_ref[0:1, :]
    rstd = moments_ref[1:2, :]
    chunks = (count_ref[0] + CHUNK - 1) // CHUNK

    def copies(c, buf):
        return [
            pltpu.make_async_copy(
                pool_ref.at[slot_ref[c * CHUNK + j]],
                held.at[buf, pl.ds(j * length, length)],
                sems.at[buf, j],
            )
            for j in range(CHUNK)
        ]

    @pl.when(chunks > 0)
    def _():
        for copy in copies(0, 0):
            copy.start()

    peak[...] = jnp.full_like(peak, LOW)
    mass[...] = jnp.zeros_like(mass)
    total[...] = jnp.zeros_like(total)
    query[tiles] = jnp.zeros((length, width), BF)
    for g in range(tiles // 3):
        rows = own_ref[pl.ds(g * 3, 3)].reshape(3 * length, width)
        normed = ((rows.astype(F32) - mean) * rstd).astype(BF)
        out = jnp.dot(normed, wq_ref[...], preferred_element_type=F32).astype(BF)
        query[pl.ds(g * 3, 3)] = out.reshape(3, length, width)

    def step(c, _):
        buf = lax.rem(c, 2)

        @pl.when(c + 1 < chunks)
        def _():
            for copy in copies(c + 1, 1 - buf):
                copy.start()

        for copy in copies(c, buf):
            copy.wait()
        normed = ((held[buf].astype(F32) - mean) * rstd).astype(BF)
        keys = jnp.dot(normed, wk_ref[...], preferred_element_type=F32).astype(BF)
        values = jnp.dot(normed, wv_ref[...], preferred_element_type=F32).astype(BF)
        done = []
        for j in range(CHUNK):
            t = row_ref[c * CHUNK + j]
            part = slice(j * length, (j + 1) * length)
            scores = lax.dot_general(
                query[t], keys[part], (((1,), (1,)), ((), ())), preferred_element_type=F32
            ) * scale
            top = jnp.max(scores, axis=1, keepdims=True)
            weights = jnp.exp(scores - top).astype(BF)
            summed = jnp.sum(weights.astype(F32), axis=1, keepdims=True)
            mixed = jnp.dot(weights, values[part], preferred_element_type=F32)
            done.append((t, top, summed, mixed))
        for t, top, summed, mixed in done:
            before = peak[t]
            after = jnp.maximum(before, top)
            keep = jnp.exp(before - after)
            gain = jnp.exp(top - after)
            peak[t] = after
            mass[t] = mass[t] * keep + gain * summed
            for b in range(blocks):
                at = slice(b * lanes, (b + 1) * lanes)
                total[t, :, at] = total[t, :, at] * keep + mixed[:, at] * gain
        return 0

    lax.fori_loop(0, chunks, step, 0)

    index = lax.broadcasted_iota(jnp.int32, (16, width), 0)
    for g in range(tiles // 3):
        notes = jnp.zeros((16, width), F32)
        for i in range(3):
            t = g * 3 + i
            some = mass[t] > 0.0
            inverse = jnp.where(some, 1.0 / jnp.where(some, mass[t], 1.0), 0.0)
            for b in range(blocks):
                at = slice(b * lanes, (b + 1) * lanes)
                out_ref[g, i * length : (i + 1) * length, at] = (total[t, :, at] * inverse).astype(BF)
            level = jnp.where(some, peak[t] + jnp.log(jnp.where(some, mass[t], 1.0)), LOW)
            row = level.T[0:1, :]
            line = jnp.concatenate(split_rows(row) + [jnp.zeros_like(row)], axis=1)
            notes = jnp.where(index == i, line, notes)
        out_ref[g, 3 * length : 3 * length + 16, :] = notes.astype(BF)


def merge_kernel(parts_ref, w_ref, out_ref):
    parts, _, width = parts_ref.shape
    lanes = 128
    length = lanes
    blocks = width // lanes
    lines = [parts_ref[y, 3 * length : 3 * length + 16, :].astype(F32) for y in range(parts)]
    for i in range(3):
        levels = []
        for y in range(parts):
            line = lines[y][i : i + 1, :]
            row = line[:, 0:lanes] + line[:, lanes : 2 * lanes] + line[:, 2 * lanes : 3 * lanes]
            levels.append(jnp.broadcast_to(row, (lanes, lanes)).T)
        top = levels[0]
        for level in levels[1:]:
            top = jnp.maximum(top, level)
        factors = [jnp.exp(level - top) for level in levels]
        whole = factors[0]
        for factor in factors[1:]:
            whole = whole + factor
        mixed = []
        for b in range(blocks):
            at = slice(b * lanes, (b + 1) * lanes)
            summed = jnp.zeros((length, lanes), F32)
            for y in range(parts):
                piece = parts_ref[y, i * length : (i + 1) * length, at].astype(F32)
                summed = summed + factors[y] * piece
            mixed.append((summed / whole).astype(BF))
        attended = jnp.concatenate(mixed, axis=1)
        result = jnp.dot(attended, w_ref[...], preferred_element_type=F32).astype(BF)
        for y in range(parts):
            out_ref[y, i * length : (i + 1) * length, :] = result[:, y * lanes : (y + 1) * lanes]


def on_device(tokens, w_query, w_key, w_value, w_out, key_owner, key_local):
    tiles, length, width = tokens.shape
    parts = lax.axis_size("pair")
    keys = key_owner.shape[2]
    part = lax.axis_index("pair")
    share = tiles // parts
    mine = lax.dynamic_slice_in_dim(tokens, part * share, share, 0)
    pool = lax.all_gather(mine, TILE, tiled=True)

    grouped = mine.astype(F32).reshape(share * length, GROUPS, width // GROUPS)
    sums = jnp.concatenate([jnp.sum(grouped, axis=(0, 2)), jnp.sum(grouped * grouped, axis=(0, 2))])
    for axis in ("core", "x", "pair", "z"):
        sums = lax.psum(sums, axis)
    count = tiles * lax.axis_size(TILE) * length * (width // GROUPS)
    mean = sums[:GROUPS] / count
    var = sums[GROUPS:] / count - mean * mean
    moments = jnp.stack([mean, lax.rsqrt(var + EPS)])
    moments = jnp.broadcast_to(moments[:, :, None], (2, GROUPS, width // GROUPS)).reshape(2, width)

    listed = lax.all_gather(key_owner[0] * 16 + key_local[0], "pair")
    owner, local = listed // 16, listed % 16
    code = jnp.where(local // share == part, owner * share + local % share, -1).reshape(-1)
    w_full = lax.all_gather(w_out, "pair", axis=1, tiled=True)

    entries = tiles * parts * keys
    smem = pl.BlockSpec(memory_space=pltpu.SMEM)
    vmem = pl.BlockSpec(memory_space=pltpu.VMEM)
    slots, rows, total_count = pl.pallas_call(
        lambda *refs: plan_kernel(tiles, parts, keys, *refs),
        out_shape=[jax.ShapeDtypeStruct((entries + 2 * CHUNK,), jnp.int32)] * 2
        + [jax.ShapeDtypeStruct((1,), jnp.int32)],
        in_specs=[smem],
        out_specs=[smem] * 3,
        name="plan",
    )(code)

    rows_out = share * length + 16
    partial = pl.pallas_call(
        attend_kernel,
        out_shape=jax.ShapeDtypeStruct((parts, rows_out, width), BF),
        in_specs=[smem] * 3 + [vmem] * 5 + [pl.BlockSpec(memory_space=pl.ANY)],
        out_specs=vmem,
        scratch_shapes=[
            pltpu.VMEM((2, CHUNK * length, width), BF),
            pltpu.VMEM((tiles + 1, length, width), BF),
            pltpu.VMEM((tiles + 1, length, 128), F32),
            pltpu.VMEM((tiles + 1, length, 128), F32),
            pltpu.VMEM((tiles + 1, length, width), F32),
            pltpu.SemaphoreType.DMA((2, CHUNK)),
        ],
        name="attend",
    )(total_count, slots, rows, tokens, moments, w_query, w_key, w_value, pool)

    swapped = lax.all_to_all(partial, "pair", split_axis=0, concat_axis=0, tiled=True)
    result = pl.pallas_call(
        merge_kernel,
        out_shape=jax.ShapeDtypeStruct((parts, share * length, width // parts), BF),
        in_specs=[vmem] * 2,
        out_specs=vmem,
        name="merge",
    )(swapped, w_full)
    result = lax.all_to_all(result, "pair", split_axis=0, concat_axis=0, tiled=True)
    return result.reshape(tiles, length, width // parts)


def solution(mesh):
    finer = Mesh(mesh.devices.reshape(4, 8, 2, 4), TILE + ("pair",))
    return jax.shard_map(
        on_device,
        mesh=finer,
        in_specs=(
            P(TILE, None, None),
            P(),
            P(),
            P(),
            P(None, "pair"),
            P("pair", TILE, None),
            P("pair", TILE, None),
        ),
        out_specs=P(TILE, None, "pair"),
        check_vma=False,
    )
```

```python
import math

import jax
import jax.numpy as jnp
from jax import lax
from jax.experimental import pallas as pl
from jax.experimental.pallas import tpu as pltpu
from jax.sharding import Mesh
from jax.sharding import PartitionSpec as P

GROUPS = 32
EPS = 1e-06
CHUNK = 4
LOW = -1e30
LATE = 1024
BF = jnp.bfloat16
F32 = jnp.float32
TILE = ("x", "z", "core")


def plan_kernel(tiles, code_ref, slot_ref, row_ref, count_ref):
    size = slot_ref.shape[1]
    per_tile = code_ref.shape[0] // tiles

    def clear(i, _):
        for part in range(2):
            slot_ref[part, i] = 0
            row_ref[part, i] = tiles
        return 0

    lax.fori_loop(0, size, clear, 0)

    def one_tile(t, counts):
        early, late = counts
        for e in range(per_tile):
            code = code_ref[t * per_tile + e]
            is_early = jnp.logical_and(code >= 0, code < LATE)
            is_late = code >= LATE
            slot_ref[0, early] = jnp.where(is_early, code, 0)
            row_ref[0, early] = jnp.where(is_early, t, tiles)
            slot_ref[1, late] = jnp.where(is_late, code - LATE, 0)
            row_ref[1, late] = jnp.where(is_late, t, tiles)
            early = early + is_early.astype(jnp.int32)
            late = late + is_late.astype(jnp.int32)
        return early, late

    early, late = lax.fori_loop(0, tiles, one_tile, (jnp.int32(0), jnp.int32(0)))
    count_ref[0] = early
    count_ref[1] = late


def split_rows(x):
    high = x.astype(BF)
    rest = x - high.astype(F32)
    mid = rest.astype(BF)
    low = (rest - mid.astype(F32)).astype(BF)
    return [part.astype(F32) for part in (high, mid, low)]


def attend_kernel(
    last, count_ref, slot_ref, row_ref, moments_ref, wk_ref, wv_ref,
    pool_0, pool_1, pool_2, pool_3, *rest,
):
    pools = (pool_0, pool_1, pool_2, pool_3)
    if last:
        query, peak_0, mass_0, total_0, out_ref, peak, mass, total, held, sems = rest
    else:
        own_ref, wq_ref, query, peak, mass, total, held, sems = rest
    tiles = query.shape[0] - 1
    length, width = query.shape[1:]
    lanes = peak.shape[2]
    blocks = width // lanes
    scale = 1.0 / math.sqrt(width)
    mean = moments_ref[0:1, :]
    rstd = moments_ref[1:2, :]
    which = int(last)
    chunks = (count_ref[which] + CHUNK - 1) // CHUNK

    def copy_of(pool, slot, buf, j):
        return pltpu.make_async_copy(
            pool.at[slot], held.at[buf, pl.ds(j * length, length)], sems.at[buf, j]
        )

    def start(c, buf):
        for j in range(CHUNK):
            code = slot_ref[which, c * CHUNK + j]
            source, slot = code // 64, lax.rem(code, 64)
            for k, pool in enumerate(pools):
                @pl.when(source == k)
                def _():
                    copy_of(pool, slot, buf, j).start()

    @pl.when(chunks > 0)
    def _():
        start(0, 0)

    peak[...] = jnp.full_like(peak, LOW)
    mass[...] = jnp.zeros_like(mass)
    total[...] = jnp.zeros_like(total)
    if not last:
        query[tiles] = jnp.zeros((length, width), BF)
        for g in range(tiles // 3):
            rows = own_ref[pl.ds(g * 3, 3)].reshape(3 * length, width)
            normed = ((rows.astype(F32) - mean) * rstd).astype(BF)
            out = jnp.dot(normed, wq_ref[...], preferred_element_type=F32).astype(BF)
            query[pl.ds(g * 3, 3)] = out.reshape(3, length, width)

    def step(c, _):
        buf = lax.rem(c, 2)

        @pl.when(c + 1 < chunks)
        def _():
            start(c + 1, 1 - buf)

        for j in range(CHUNK):
            copy_of(pools[0], 0, buf, j).wait()
        normed = ((held[buf].astype(F32) - mean) * rstd).astype(BF)
        keys = jnp.dot(normed, wk_ref[...], preferred_element_type=F32).astype(BF)
        values = jnp.dot(normed, wv_ref[...], preferred_element_type=F32).astype(BF)
        done = []
        for j in range(CHUNK):
            t = row_ref[which, c * CHUNK + j]
            part = slice(j * length, (j + 1) * length)
            scores = lax.dot_general(
                query[t], keys[part], (((1,), (1,)), ((), ())), preferred_element_type=F32
            ) * scale
            top = jnp.max(scores, axis=1, keepdims=True)
            weights = jnp.exp(scores - top).astype(BF)
            summed = jnp.sum(weights.astype(F32), axis=1, keepdims=True)
            mixed = jnp.dot(weights, values[part], preferred_element_type=F32)
            done.append((t, top, summed, mixed))
        for t, top, summed, mixed in done:
            before = peak[t]
            after = jnp.maximum(before, top)
            keep = jnp.exp(before - after)
            gain = jnp.exp(top - after)
            peak[t] = after
            mass[t] = mass[t] * keep + gain * summed
            for b in range(blocks):
                at = slice(b * lanes, (b + 1) * lanes)
                total[t, :, at] = total[t, :, at] * keep + mixed[:, at] * gain
        return 0

    lax.fori_loop(0, chunks, step, 0)
    if not last:
        return

    index = lax.broadcasted_iota(jnp.int32, (16, width), 0)
    for g in range(tiles // 3):
        notes = jnp.zeros((16, width), F32)
        for i in range(3):
            t = g * 3 + i
            top = jnp.maximum(peak[t], peak_0[t])
            new = jnp.exp(peak[t] - top)
            old = jnp.exp(peak_0[t] - top)
            weight = mass[t] * new + mass_0[t] * old
            some = weight > 0.0
            inverse = jnp.where(some, 1.0 / jnp.where(some, weight, 1.0), 0.0)
            new = new * inverse
            old = old * inverse
            for b in range(blocks):
                at = slice(b * lanes, (b + 1) * lanes)
                mixed = total[t, :, at] * new + total_0[t, :, at] * old
                out_ref[g, i * length : (i + 1) * length, at] = mixed.astype(BF)
            level = jnp.where(some, top + jnp.log(jnp.where(some, weight, 1.0)), LOW)
            row = level.T[0:1, :]
            line = jnp.concatenate(split_rows(row) + [jnp.zeros_like(row)], axis=1)
            notes = jnp.where(index == i, line, notes)
        out_ref[g, 3 * length : 3 * length + 16, :] = notes.astype(BF)


def merge_kernel(me_ref, parts_ref, w0_ref, w1_ref, w2_ref, w3_ref, out_ref):
    parts, _, width = parts_ref.shape
    lanes = 128
    length = lanes
    blocks = width // lanes
    lines = [parts_ref[y, 3 * length : 3 * length + 16, :].astype(F32) for y in range(parts)]
    for i in range(3):
        levels = []
        for y in range(parts):
            line = lines[y][i : i + 1, :]
            row = line[:, 0:lanes] + line[:, lanes : 2 * lanes] + line[:, 2 * lanes : 3 * lanes]
            levels.append(jnp.broadcast_to(row, (lanes, lanes)).T)
        top = levels[0]
        for level in levels[1:]:
            top = jnp.maximum(top, level)
        factors = [jnp.exp(level - top) for level in levels]
        whole = factors[0]
        for factor in factors[1:]:
            whole = whole + factor
        mixed = []
        for b in range(blocks):
            at = slice(b * lanes, (b + 1) * lanes)
            summed = jnp.zeros((length, lanes), F32)
            for y in range(parts):
                piece = parts_ref[y, i * length : (i + 1) * length, at].astype(F32)
                summed = summed + factors[y] * piece
            mixed.append((summed / whole).astype(BF))
        attended = jnp.concatenate(mixed, axis=1)
        for s, w_ref in enumerate((w0_ref, w1_ref, w2_ref, w3_ref)):
            result = jnp.dot(attended, w_ref[0:width, :], preferred_element_type=F32).astype(BF)
            out_ref[lax.rem(me_ref[0] + parts - s, parts), i * length : (i + 1) * length, :] = result


def shifted(x, first, second):
    pairs = []
    for c, move in enumerate((first, second)):
        if move is not None:
            for i in range(4):
                for k in range(8):
                    target = ((i + move[0]) % 4 * 8 + (k + move[1]) % 8) * 2 + c
                    pairs.append(((i * 8 + k) * 2 + c, target))
    return lax.ppermute(x, TILE, pairs)


def exchanged(x):
    return lax.ppermute(x, "core", [(0, 1), (1, 0)])


def gathered(mine, is_first, sums_of, plan_of, attend_of):
    half = mine.shape[1] // 2
    join = lambda *parts: jnp.concatenate(parts)
    right, left = ((1, 0), (0, 1)), ((-1, 0), (0, -1))
    p1, m1 = shifted(mine, *right), shifted(mine, *left)
    p2, m2 = shifted(p1, *right), shifted(m1, *left)
    near = join(mine, p1, m1, p2)
    right, left = ((0, 1), (1, 0)), ((0, -1), (-1, 0))
    p3, m3 = shifted(p2, None, (0, 1)), shifted(m2, None, (0, -1))
    p5, m5 = shifted(near, *right), shifted(near, *left)
    p4, m4 = shifted(p3[:, :half], None, (0, 1)), shifted(m3[:, half:], None, (0, -1))
    far = join(m2, p3, m3, jnp.concatenate([p4, m4], axis=1))
    pool_1 = join(near, far, p5, m5)
    moments = sums_of()
    p5, m5, far, moments = lax.optimization_barrier((p5, m5, far, moments))
    p6 = shifted(jnp.where(is_first, p5, far), *right)
    m6 = shifted(jnp.where(is_first, m5, far), *left)
    pool_2 = join(p6, m6)
    lists = plan_of()
    early = [pool_1, exchanged(pool_1), pool_2, exchanged(pool_2)]
    p6, m6, lists = lax.optimization_barrier((p6, m6, lists))
    p7 = shifted(jnp.where(is_first, p6, p5), *right)
    m7 = shifted(m6, *left)
    pool_3 = join(p7, m7)
    state = attend_of(moments, lists, early)
    others_3 = exchanged(pool_3)
    cut = p7.shape[0] // 2
    p7, m7, state = lax.optimization_barrier((p7, m7, state))
    p8, m8 = shifted(p7[:cut], (0, 1), None), shifted(m7[cut:], (0, -1), None)
    pool_4 = join(p8, m8)
    return moments, lists, state, [pool_3, others_3, pool_4, exchanged(pool_4)]


def placed(owner, local, share):
    me = [lax.axis_index(axis) for axis in TILE]
    dx = (me[0] - owner // 16) % 4
    dz = (me[1] - owner // 2 % 8) % 8
    core = owner % 2
    pick = lambda table, index: sum(jnp.where(index == i, v, 0) for i, v in enumerate(table))
    at_x = pick((0, 1, 3, 2), dx)
    at_z = pick((0, 1, 3, 5, 7, 6, 4, 2), dz)
    pool_a = pick((0, 0, 1, 2, 3, 2, 1, 0), dz)
    unit_a = at_x + pick((0, 8, 0, 0, 0, 4, 4, 12), dz)
    near = at_z < 4
    pool_b = jnp.where(dx == 0, 0, jnp.where(dx == 2, 2, jnp.where(near, 0, 1)))
    unit_b = jnp.where(
        jnp.logical_or(dx == 0, dx == 2),
        at_z,
        jnp.where(near, 8 + at_z, at_z - 4) + jnp.where(dx == 3, 4, 0),
    )
    pool = jnp.where(core == 0, pool_a, pool_b)
    unit = jnp.where(core == 0, unit_a, unit_b)
    source = (pool % 2) * 2 + jnp.where(core == me[2], 0, 1)
    return pool // 2 * LATE + source * 64 + unit * share + local % share


def on_device(tokens, w_query, w_key, w_value, w_out, key_owner, key_local):
    tiles, length, width = tokens.shape
    parts = lax.axis_size("pair")
    keys = key_owner.shape[2]
    part = lax.axis_index("pair")
    share = tiles // parts
    mine = lax.dynamic_slice_in_dim(tokens, part * share, share, 0)
    smem = pl.BlockSpec(memory_space=pltpu.SMEM)
    vmem = pl.BlockSpec(memory_space=pltpu.VMEM)
    anywhere = pl.BlockSpec(memory_space=pl.ANY)
    entries = tiles * keys

    names = jnp.concatenate([key_owner.reshape(-1), key_local.reshape(-1)]).astype(BF)
    names = jnp.zeros((16, w_out.shape[1]), BF).at[0, : names.shape[0]].set(names)
    bundle = jnp.concatenate([w_out, names])
    bundles = [bundle] + [
        lax.ppermute(bundle, "pair", [(i, (i + s) % parts) for i in range(parts)]) for s in range(1, parts)
    ]

    def sums_of():
        grouped = tokens.astype(F32).reshape(tiles * length, GROUPS, width // GROUPS)
        sums = jnp.concatenate([jnp.sum(grouped, axis=(0, 2)), jnp.sum(grouped * grouped, axis=(0, 2))])
        for axis, size in (("core", 2), ("x", 4), ("z", 8)):
            step = 1
            while step < size:
                sums = sums + lax.ppermute(sums, axis, [(i, i ^ step) for i in range(size)])
                step *= 2
        count = tiles * lax.axis_size(TILE) * length * (width // GROUPS)
        mean = sums[:GROUPS] / count
        var = sums[GROUPS:] / count - mean * mean
        moments = jnp.stack([mean, lax.rsqrt(var + EPS)])
        return jnp.broadcast_to(moments[:, :, None], (2, GROUPS, width // GROUPS)).reshape(2, width)

    def plan_of():
        listed = jnp.stack([b[width, : 2 * entries] for b in bundles]).astype(jnp.int32)
        owner = listed[:, :entries].reshape(parts, tiles, keys).transpose(1, 0, 2).reshape(-1)
        local = listed[:, entries:].reshape(parts, tiles, keys).transpose(1, 0, 2).reshape(-1)
        code = jnp.where(local // share == part, placed(owner, local, share), -1)
        size = parts * entries + 2 * CHUNK
        slots, rows, counts = pl.pallas_call(
            lambda *refs: plan_kernel(tiles, *refs),
            out_shape=[jax.ShapeDtypeStruct((2, size), jnp.int32)] * 2
            + [jax.ShapeDtypeStruct((2,), jnp.int32)],
            in_specs=[smem],
            out_specs=[smem] * 3,
            name="plan",
        )(code)
        return counts, slots, rows

    state = [
        jax.ShapeDtypeStruct((tiles + 1, length, width), BF),
        jax.ShapeDtypeStruct((tiles + 1, length, 128), F32),
        jax.ShapeDtypeStruct((tiles + 1, length, 128), F32),
        jax.ShapeDtypeStruct((tiles + 1, length, width), F32),
    ]
    held = [pltpu.VMEM((2, CHUNK * length, width), BF), pltpu.SemaphoreType.DMA((2, CHUNK))]

    def cost(n):
        flops = n * length * width * (4 * width + 4 * length)
        return pl.CostEstimate(flops=flops, transcendentals=0, bytes_accessed=n * 2 * length * width)

    def attend_of(moments, lists, pools):
        return pl.pallas_call(
            lambda *refs: attend_kernel(False, *refs),
            out_shape=state,
            in_specs=[smem] * 3 + [vmem] * 3 + [anywhere] * 4 + [vmem] * 2,
            out_specs=[vmem] * 4,
            scratch_shapes=held,
            cost_estimate=cost(80),
            name="attend_early",
        )(*lists, moments, w_key, w_value, *pools, tokens, w_query)

    is_first = lax.axis_index("core") == 0
    moments, lists, first, pools = gathered(mine, is_first, sums_of, plan_of, attend_of)
    partial = pl.pallas_call(
        lambda *refs: attend_kernel(True, *refs),
        out_shape=jax.ShapeDtypeStruct((parts, share * length + 16, width), BF),
        in_specs=[smem] * 3 + [vmem] * 3 + [anywhere] * 4 + [vmem] * 4,
        out_specs=vmem,
        scratch_shapes=[pltpu.VMEM(s.shape, s.dtype) for s in state[1:]] + held,
        cost_estimate=cost(30),
        name="attend_late",
    )(*lists, moments, w_key, w_value, *pools, *first)

    swapped = lax.all_to_all(partial, "pair", split_axis=0, concat_axis=0, tiled=True)
    result = pl.pallas_call(
        merge_kernel,
        out_shape=jax.ShapeDtypeStruct((parts, share * length, width // parts), BF),
        in_specs=[smem] + [vmem] * 5,
        out_specs=vmem,
        name="merge",
    )(jnp.full((1,), part, jnp.int32), swapped, *bundles)
    result = lax.all_to_all(result, "pair", split_axis=0, concat_axis=0, tiled=True)
    return result.reshape(tiles, length, width // parts)


def solution(mesh):
    finer = Mesh(mesh.devices.reshape(4, 8, 2, 4), TILE + ("pair",))
    return jax.shard_map(
        on_device,
        mesh=finer,
        in_specs=(
            P(TILE, None, None),
            P(),
            P(),
            P(),
            P(None, "pair"),
            P("pair", TILE, None),
            P("pair", TILE, None),
        ),
        out_specs=P(TILE, None, "pair"),
        check_vma=False,
    )
```

```python
import math

import jax
import jax.numpy as jnp
from jax import lax
from jax.experimental import pallas as pl
from jax.experimental.pallas import tpu as pltpu
from jax.sharding import Mesh
from jax.sharding import PartitionSpec as P

GROUPS = 32
EPS = 1e-06
CHUNK = 4
LOW = -1e30
STAGE = 1024
KERNELS = 2
BF = jnp.bfloat16
F32 = jnp.float32
TILE = ("x", "z", "core")


def bundle_kernel(w_ref, owner_ref, local_ref, out_ref, names):
    depth = w_ref.shape[0]
    keys, tiles = owner_ref.shape
    out_ref[0:depth, :] = w_ref[...]
    names[...] = jnp.zeros_like(names)
    names[0:keys, 0:tiles] = owner_ref[...].astype(F32)
    names[keys : 2 * keys, 0:tiles] = local_ref[...].astype(F32)
    out_ref[depth : depth + 16, :] = names[...].astype(BF)


def places(me_ref, owner, local):
    core = owner & 1
    share = (local * 11) >> 5
    at = local - 3 * share
    turn = 1 - 2 * core
    steps_x = (turn * (me_ref[0] - (owner >> 4))) & 3
    steps_z = (turn * (me_ref[1] - ((owner >> 1) & 7))) & 7
    early = jnp.where(core == me_ref[2], 0, 128) + steps_z * 4 + steps_x
    code = jnp.where(at == 2, early, STAGE + owner * 2 + at)
    return jnp.where(share == me_ref[3], code, KERNELS * STAGE)


def plan_kernel(tiles, keys, me_ref, b0_ref, b1_ref, b2_ref, b3_ref, slot_ref, row_ref, count_ref, codes, table):
    bundles = (b0_ref, b1_ref, b2_ref, b3_ref)
    for s, b_ref in enumerate(bundles):
        depth = b_ref.shape[0] - 16
        names = b_ref[depth : depth + 16, :].astype(F32).astype(jnp.int32)
        codes[s * keys : (s + 1) * keys, :] = places(me_ref, names[0:keys, :], names[keys : 2 * keys, :])
    pltpu.sync_copy(codes, table)
    lists = slot_ref.shape[0]
    for k in range(lists):
        count_ref[k] = 0

    def one_tile(t, _):
        for e in range(len(bundles) * keys):
            code = table[e, t]
            k = code >> 10
            n = count_ref[k]
            slot_ref[k, n] = code & (STAGE - 1)
            row_ref[k, n] = t
            count_ref[k] = n + 1
        return 0

    lax.fori_loop(0, tiles, one_tile, 0)
    for k in range(lists):
        n = count_ref[k]
        for i in range(CHUNK):
            slot_ref[k, n + i] = 0
            row_ref[k, n + i] = tiles


def split_rows(x):
    high = x.astype(BF)
    rest = x - high.astype(F32)
    mid = rest.astype(BF)
    low = (rest - mid.astype(F32)).astype(BF)
    return [part.astype(F32) for part in (high, mid, low)]


def attend_kernel(
    which, count_ref, slot_ref, row_ref, moments_ref, wk_ref, wv_ref, *rest,
):
    begin, last = which == 0, which == KERNELS - 1
    count = 2 if begin else 1
    pools, rest = rest[:count], rest[count:]
    if begin:
        own_ref, wq_ref, query, peak, mass, total, held, sems = rest
    else:
        query, peak_0, mass_0, total_0, out_ref, peak, mass, total, held, sems = rest
    tiles = query.shape[0] - 1
    length, width = query.shape[1:]
    lanes = peak.shape[2]
    blocks = width // lanes
    scale = 1.0 / math.sqrt(width)
    mean = moments_ref[0:1, :]
    rstd = moments_ref[1:2, :]
    chunks = (count_ref[which] + CHUNK - 1) // CHUNK

    def copy_of(pool, slot, buf, j):
        return pltpu.make_async_copy(
            pool.at[slot], held.at[buf, pl.ds(j * length, length)], sems.at[buf, j]
        )

    def start(c, buf):
        for j in range(CHUNK):
            code = slot_ref[which, c * CHUNK + j]
            source, slot = code >> 7, code & 127

            def among(low, high):
                if high - low == 1:
                    copy_of(pools[low], slot, buf, j).start()
                    return
                middle = (low + high) // 2
                pl.when(source < middle)(lambda: among(low, middle))
                pl.when(source >= middle)(lambda: among(middle, high))

            among(0, len(pools))

    @pl.when(chunks > 0)
    def _():
        start(0, 0)

    peak[...] = jnp.full_like(peak, LOW)
    mass[...] = jnp.zeros_like(mass)
    total[...] = jnp.zeros_like(total)
    if begin:
        query[tiles] = jnp.zeros((length, width), BF)
        for g in range(tiles // 3):
            rows = own_ref[pl.ds(g * 3, 3)].reshape(3 * length, width)
            normed = ((rows.astype(F32) - mean) * rstd).astype(BF)
            out = jnp.dot(normed, wq_ref[...], preferred_element_type=F32).astype(BF)
            query[pl.ds(g * 3, 3)] = out.reshape(3, length, width)

    def step(c, _):
        buf = lax.rem(c, 2)

        @pl.when(c + 1 < chunks)
        def _():
            start(c + 1, 1 - buf)

        for j in range(CHUNK):
            copy_of(pools[0], 0, buf, j).wait()
        normed = ((held[buf].astype(F32) - mean) * rstd).astype(BF)
        keys = jnp.dot(normed, wk_ref[...], preferred_element_type=F32).astype(BF)
        values = jnp.dot(normed, wv_ref[...], preferred_element_type=F32).astype(BF)
        done = []
        for j in range(CHUNK):
            t = row_ref[which, c * CHUNK + j]
            part = slice(j * length, (j + 1) * length)
            scores = lax.dot_general(
                query[t], keys[part], (((1,), (1,)), ((), ())), preferred_element_type=F32
            ) * scale
            top = jnp.max(scores, axis=1, keepdims=True)
            weights = jnp.exp(scores - top).astype(BF)
            summed = jnp.sum(weights.astype(F32), axis=1, keepdims=True)
            mixed = jnp.dot(weights, values[part], preferred_element_type=F32)
            done.append((t, top, summed, mixed))
        for t, top, summed, mixed in done:
            before = peak[t]
            after = jnp.maximum(before, top)
            keep = jnp.exp(before - after)
            gain = jnp.exp(top - after)
            peak[t] = after
            mass[t] = mass[t] * keep + gain * summed
            for b in range(blocks):
                at = slice(b * lanes, (b + 1) * lanes)
                total[t, :, at] = total[t, :, at] * keep + mixed[:, at] * gain
        return 0

    lax.fori_loop(0, chunks, step, 0)
    if not last:
        return

    index = lax.broadcasted_iota(jnp.int32, (16, width), 0)
    for g in range(tiles // 3):
        notes = jnp.zeros((16, width), F32)
        for i in range(3):
            t = g * 3 + i
            top = jnp.maximum(peak[t], peak_0[t])
            new = jnp.exp(peak[t] - top)
            old = jnp.exp(peak_0[t] - top)
            weight = mass[t] * new + mass_0[t] * old
            some = weight > 0.0
            inverse = jnp.where(some, 1.0 / jnp.where(some, weight, 1.0), 0.0)
            new = new * inverse
            old = old * inverse
            for b in range(blocks):
                at = slice(b * lanes, (b + 1) * lanes)
                mixed = total[t, :, at] * new + total_0[t, :, at] * old
                out_ref[g, i * length : (i + 1) * length, at] = mixed.astype(BF)
            level = jnp.where(some, top + jnp.log(jnp.where(some, weight, 1.0)), LOW)
            row = level.T[0:1, :]
            line = jnp.concatenate(split_rows(row) + [jnp.zeros_like(row)], axis=1)
            notes = jnp.where(index == i, line, notes)
        out_ref[g, 3 * length : 3 * length + 16, :] = notes.astype(BF)


def merge_kernel(me_ref, parts_ref, w0_ref, w1_ref, w2_ref, w3_ref, out_ref):
    parts, _, width = parts_ref.shape
    lanes = 128
    length = lanes
    blocks = width // lanes
    lines = [parts_ref[y, 3 * length : 3 * length + 16, :].astype(F32) for y in range(parts)]
    for i in range(3):
        levels = []
        for y in range(parts):
            line = lines[y][i : i + 1, :]
            row = line[:, 0:lanes] + line[:, lanes : 2 * lanes] + line[:, 2 * lanes : 3 * lanes]
            levels.append(jnp.broadcast_to(row, (lanes, lanes)).T)
        top = levels[0]
        for level in levels[1:]:
            top = jnp.maximum(top, level)
        factors = [jnp.exp(level - top) for level in levels]
        whole = factors[0]
        for factor in factors[1:]:
            whole = whole + factor
        mixed = []
        for b in range(blocks):
            at = slice(b * lanes, (b + 1) * lanes)
            summed = jnp.zeros((length, lanes), F32)
            for y in range(parts):
                piece = parts_ref[y, i * length : (i + 1) * length, at].astype(F32)
                summed = summed + factors[y] * piece
            mixed.append((summed / whole).astype(BF))
        attended = jnp.concatenate(mixed, axis=1)
        for s, w_ref in enumerate((w0_ref, w1_ref, w2_ref, w3_ref)):
            result = jnp.dot(attended, w_ref[0:width, :], preferred_element_type=F32).astype(BF)
            out_ref[lax.rem(me_ref[0] + parts - s, parts), i * length : (i + 1) * length, :] = result


def shifted(x, first, second):
    pairs = []
    for c, move in enumerate((first, second)):
        if move is not None:
            for i in range(4):
                for k in range(8):
                    target = ((i + move[0]) % 4 * 8 + (k + move[1]) % 8) * 2 + c
                    pairs.append(((i * 8 + k) * 2 + c, target))
    return lax.ppermute(x, TILE, pairs)


def gathered(mine):
    two = jnp.concatenate([mine, shifted(mine, (1, 0), (-1, 0))])
    held = jnp.concatenate([two, shifted(two, (2, 0), (-2, 0))])
    parts = [held]
    for _ in range(7):
        held = shifted(held, (0, 1), (0, -1))
        parts.append(held)
    pool = jnp.concatenate(parts)
    return pool, lax.ppermute(pool, "core", [(0, 1), (1, 0)])


def on_device(tokens, w_query, w_key, w_value, w_out, key_owner, key_local):
    tiles, length, width = tokens.shape
    parts = lax.axis_size("pair")
    keys = key_owner.shape[2]
    part = lax.axis_index("pair")
    share = tiles // parts
    pool = lax.all_gather(lax.dynamic_slice_in_dim(tokens, part * share, share - 1, 0), TILE, tiled=True)
    early = gathered(lax.dynamic_slice_in_dim(tokens, part * share + share - 1, 1, 0))
    smem = pl.BlockSpec(memory_space=pltpu.SMEM)
    vmem = pl.BlockSpec(memory_space=pltpu.VMEM)
    anywhere = pl.BlockSpec(memory_space=pl.ANY)
    entries = tiles * keys

    bundle = pl.pallas_call(
        bundle_kernel,
        out_shape=jax.ShapeDtypeStruct((width + 16, w_out.shape[1]), BF),
        in_specs=[vmem] * 3,
        out_specs=vmem,
        scratch_shapes=[pltpu.VMEM((16, w_out.shape[1]), F32)],
        name="bundle",
    )(w_out, key_owner[0].T, key_local[0].T)
    bundles = [bundle]
    for s in range(1, parts):
        bundles.append(lax.ppermute(bundle, "pair", [(i, (i + s) % parts) for i in range(parts)]))

    grouped = tokens.astype(F32).reshape(tiles * length, GROUPS, width // GROUPS)
    sums = jnp.concatenate([jnp.sum(grouped, axis=(0, 2)), jnp.sum(grouped * grouped, axis=(0, 2))])
    for axis, n in (("core", 2), ("x", 4), ("z", 8)):
        step = 1
        while step < n:
            sums = sums + lax.ppermute(sums, axis, [(i, i ^ step) for i in range(n)])
            step *= 2
    count = tiles * lax.axis_size(TILE) * length * (width // GROUPS)
    mean = sums[:GROUPS] / count
    var = sums[GROUPS:] / count - mean * mean
    moments = jnp.stack([mean, lax.rsqrt(var + EPS)])
    moments = jnp.broadcast_to(moments[:, :, None], (2, GROUPS, width // GROUPS)).reshape(2, width)

    me = jnp.stack([lax.axis_index(axis) for axis in TILE + ("pair",)]).astype(jnp.int32)
    size = parts * entries + 2 * CHUNK
    lists = pl.pallas_call(
        lambda *refs: plan_kernel(tiles, keys, *refs),
        out_shape=[jax.ShapeDtypeStruct((KERNELS + 1, size), jnp.int32)] * 2
        + [jax.ShapeDtypeStruct((KERNELS + 1,), jnp.int32)],
        in_specs=[smem] + [vmem] * 4,
        out_specs=[smem] * 3,
        scratch_shapes=[
            pltpu.VMEM((parts * keys, 128), jnp.int32),
            pltpu.SMEM((parts * keys, 128), jnp.int32),
        ],
        name="plan",
    )(me, *bundles)
    counts, slots, rows = lists[2], lists[0], lists[1]
    lists = (counts, slots, rows)

    state = [
        jax.ShapeDtypeStruct((tiles + 1, length, width), BF),
        jax.ShapeDtypeStruct((tiles + 1, length, 128), F32),
        jax.ShapeDtypeStruct((tiles + 1, length, 128), F32),
        jax.ShapeDtypeStruct((tiles + 1, length, width), F32),
    ]
    held = [pltpu.VMEM((2, CHUNK * length, width), BF), pltpu.SemaphoreType.DMA((2, CHUNK))]

    def cost(n):
        flops = n * length * width * (4 * width + 4 * length)
        return pl.CostEstimate(flops=flops, transcendentals=0, bytes_accessed=n * 2 * length * width)

    first = pl.pallas_call(
        lambda *refs: attend_kernel(0, *refs),
        out_shape=state,
        in_specs=[smem] * 3 + [vmem] * 3 + [anywhere] * 2 + [vmem] * 2,
        out_specs=[vmem] * 4,
        scratch_shapes=held,
        cost_estimate=cost(20),
        name="attend_early",
    )(*lists, moments, w_key, w_value, *early, tokens, w_query)
    partial = pl.pallas_call(
        lambda *refs: attend_kernel(1, *refs),
        out_shape=jax.ShapeDtypeStruct((parts, share * length + 16, width), BF),
        in_specs=[smem] * 3 + [vmem] * 3 + [anywhere] + [vmem] * 4,
        out_specs=vmem,
        scratch_shapes=[pltpu.VMEM(s.shape, s.dtype) for s in state[1:]] + held,
        cost_estimate=cost(40),
        name="attend_late",
    )(*lists, moments, w_key, w_value, pool, *first)

    swapped = lax.all_to_all(partial, "pair", split_axis=0, concat_axis=0, tiled=True)
    result = pl.pallas_call(
        merge_kernel,
        out_shape=jax.ShapeDtypeStruct((parts, share * length, width // parts), BF),
        in_specs=[smem] + [vmem] * 5,
        out_specs=vmem,
        name="merge",
    )(me[3:], swapped, *bundles)
    result = lax.all_to_all(result, "pair", split_axis=0, concat_axis=0, tiled=True)
    return result.reshape(tiles, length, width // parts)


def solution(mesh):
    finer = Mesh(mesh.devices.reshape(4, 8, 2, 4), TILE + ("pair",))

    return jax.shard_map(
        on_device,
        mesh=finer,
        in_specs=(P(TILE, None, None), P(), P(), P(), P(None, "pair"), P("pair", TILE, None), P("pair", TILE, None)),
        out_specs=P(TILE, None, "pair"),
        check_vma=False,
    )
```
